32 devices in a mesh: groups: 2 (over y), dp: 4 (over z), heads: 4 (over x, core).
Axes of the slice: x: 2, y: 2, z: 4, core: 2. Of those that a mesh axis runs over, the one named last changes fastest.
Arguments:
- queries: bfloat16 [2048, 64, 128], P(('groups', 'dp'), 'heads'), parts along dimension 0, may hold values from -41 to 41
- out_grad: bfloat16 [2048, 64, 128], P(('groups', 'dp'), 'heads'), parts along dimension 0, may hold values from -24 to 24
- self_keys: bfloat16 [2048, 8, 128], P(('groups', 'dp'), 'heads'), parts along dimension 0, may hold values from -6 to 6
- self_values: bfloat16 [2048, 8, 128], P(('groups', 'dp'), 'heads'), parts along dimension 0, may hold values from -6 to 6
- cart_keys: bfloat16 [2048, 8, 128], P('groups', 'heads'), parts along dimension 0, may hold values from -17 to 17
- cart_values: bfloat16 [2048, 8, 128], P('groups', 'heads'), parts along dimension 0, may hold values from -6 to 6
- segment_ids: int32 [8, 256], P(('groups', 'dp')), parts along dimension 0, may hold values from 0 to 1, never falling along the last dimension, each value on 1 to 192 neighbouring positions
Outputs:
- cart_grads: float32 [2048, 2, 8, 128], P(('groups', 'dp'), None, 'heads'), parts along dimension 0
- self_grads: bfloat16 [2, 2048, 8, 128], P(None, ('groups', 'dp'), 'heads'), parts along dimension 1
- query_grads: bfloat16 [2048, 8192], P(('groups', 'dp', 'heads')), parts along dimension 0
The draws below stay inside these ranges and needn't reach their ends.
There are 2 independent parts, one for each index of `groups`. The reference program is written for one: setup_inputs(seed, part) draws one part's arguments, and reference() takes and returns one part's arrays. A program takes and returns all parts, laid end to end along the dimension named above; each array names one. Nothing has to cross between parts.
Inputs may be any that keep to these rules, and one draw needn't show every extreme that they name: `segment_ids`: in each row ids never fall and both sequences occur; one sequence of a row may hold up to 192 positions.
All inputs are finite; a program needn't handle non-finite values.
Results may differ from the reference program's by a relative error of at most 0.0053.
Values may be sent and summed in bfloat16 or wider, within the bound.
A program may use at most 64 MiB of HBM per device.

```python
import math
import jax
import jax.numpy as jnp
import numpy as np
from jax import lax

H = 64
KVH = 8
DH = 128
TOK = 256
P_SIZE = 1024
ROWS = 4
TOKENS = 1024


def cart_table(key):
    normal_part = jnp.clip(jax.random.normal(jax.random.fold_in(key, 11), (P_SIZE, KVH, DH), jnp.float32), -4.0, 4.0)
    return normal_part


def draw_cart_keys(key, part):
    return cart_table(key).astype(jnp.bfloat16)


def draw_queries(key, part):
    normal_part = jnp.clip(jax.random.normal(jax.random.fold_in(key, 12), (TOKENS, H, DH), jnp.float32), -4.0, 4.0)
    return normal_part.astype(jnp.bfloat16)


def steps_of(stream_key, shape, split, least, top_value):
    gain, own = 1.0, jax.random.fold_in(stream_key, 6)
    for axis_at, parts in split:
        steps = jnp.exp(jax.random.uniform(jax.random.fold_in(own, axis_at), (parts,), jnp.float32, least / len(split), top_value / len(split)))
        gain = gain * jnp.repeat(steps, shape[axis_at] // parts).reshape([-1 if axis == axis_at else 1 for axis in range(len(shape))])
    return gain


def split_up(amount, total, limit, slope):
    loads = [(1 << 20) // math.isqrt(grade ** slope) + 1 for grade in range(2, amount + 1)]
    rest, counts = total - limit - (amount - 1), [1] * (amount - 1)
    while rest > 0:
        free = [i for i in range(amount - 1) if counts[i] < limit]
        pool, remaining = sum([loads[i] for i in free]), rest
        for i in free:
            more = min(limit - counts[i], max(1, remaining * loads[i] // pool), rest)
            counts[i] = counts[i] + more
            rest = rest - more
    return np.array([limit] + counts)


def uneven(stream_key, amount, total, bound, skew):
    if amount == 2:
        one = jax.random.randint(stream_key, (), max(1, total - bound), min(bound, total - 1) + 1)
        return jnp.stack([one, total - one])
    lengths = jnp.asarray(split_up(amount, total, bound, skew), jnp.int32)
    twos = (amount - 1) // 2
    giver, sink = lengths[1:1 + 2 * twos:2], lengths[2:2 + 2 * twos:2]
    room = jnp.minimum(giver - 1, bound - sink)
    moved = jax.random.randint(jax.random.fold_in(stream_key, 1), (twos,), 0, 1 << 20) % (room + 1)
    lengths = lengths.at[1:1 + 2 * twos:2].set(giver - moved).at[2:2 + 2 * twos:2].set(sink + moved)
    return lengths[jax.random.permutation(jax.random.fold_in(stream_key, 2), amount)]


def scatter_about(own_key, shape, scale, limit, cuts=(), dtype=jnp.bfloat16):
    drawn = scale * jax.random.normal(own_key, shape, jnp.float32)
    if cuts:
        drawn = drawn * steps_of(own_key, shape, cuts, -0.22, 0.18)
    return jnp.clip(drawn, -limit, limit).astype(dtype)


def setup_inputs(seed: int = 0, part: int = 0) -> dict:
    splits = jax.random.split(jax.random.key(seed), 8)
    own_keys = jax.random.split(jax.random.fold_in(splits[7], part), 8)
    queries = draw_queries(jax.random.fold_in(jax.random.fold_in(splits[7], part), 71), part)
    out_grad = scatter_about(own_keys[1], (TOKENS, H, DH), 4.0, 24.0, ((0, 4), (1, 4)))
    self_keys = scatter_about(own_keys[2], (TOKENS, KVH, DH), 1.0, 6.0, ((0, 4), (1, 4)))
    self_values = scatter_about(own_keys[3], (TOKENS, KVH, DH), 1.0, 6.0, ((0, 4), (1, 4)))
    cart_keys = draw_cart_keys(jax.random.fold_in(jax.random.fold_in(splits[7], part), 71), part)
    cart_values = scatter_about(own_keys[5], (P_SIZE, KVH, DH), 1.0, 6.0, ((1, 4),))
    segment_ids = jax.vmap(lambda own: jnp.searchsorted(jnp.cumsum(uneven(own, 2, TOK, TOK * 3 // 4, 0)), jnp.arange(TOK), side="right"))(jax.random.split(own_keys[6], ROWS)).reshape((ROWS, TOK)).astype(jnp.int32)
    return {"queries": queries, "out_grad": out_grad, "self_keys": self_keys, "self_values": self_values, "cart_keys": cart_keys, "cart_values": cart_values, "segment_ids": segment_ids}


masked_score = -1.0e30


def block_masks(segment_row):
    positions = jnp.arange(segment_row.shape[0])
    same_doc = segment_row[:, None] == segment_row[None, :]
    return same_doc & (positions[None, :] <= positions[:, None])


def head_block(query_rows, grad_rows, visible, cart_k, cart_v, own_k, own_v):
    token_count, block_width, head_dim = query_rows.shape
    score_scale = head_dim ** -0.5
    flat_query = query_rows.reshape(token_count * block_width, head_dim)
    flat_grad = grad_rows.reshape(token_count * block_width, head_dim)
    wide_mask = jnp.repeat(visible, block_width, axis=0)
    cart_scores = jnp.dot(flat_query, cart_k.T, preferred_element_type=jnp.float32) * score_scale
    own_scores = jnp.where(wide_mask, jnp.dot(flat_query, own_k.T, preferred_element_type=jnp.float32) * score_scale, masked_score)
    row_peak = jnp.maximum(jnp.max(cart_scores, axis=1, keepdims=True), jnp.max(own_scores, axis=1, keepdims=True))
    cart_exp = jnp.exp(cart_scores - row_peak)
    own_exp = jnp.exp(own_scores - row_peak)
    row_total = jnp.sum(cart_exp, axis=1, keepdims=True) + jnp.sum(own_exp, axis=1, keepdims=True)
    cart_prob = cart_exp / row_total
    own_prob = own_exp / row_total
    cart_dprob = jnp.dot(flat_grad, cart_v.T, preferred_element_type=jnp.float32)
    own_dprob = jnp.dot(flat_grad, own_v.T, preferred_element_type=jnp.float32)
    center = jnp.sum(cart_prob * cart_dprob, axis=1, keepdims=True) + jnp.sum(own_prob * own_dprob, axis=1, keepdims=True)
    cart_ds = (cart_prob * (cart_dprob - center)).astype(jnp.bfloat16)
    own_ds = (own_prob * (own_dprob - center)).astype(jnp.bfloat16)
    query_grad = (jnp.dot(cart_ds, cart_k, preferred_element_type=jnp.float32) + jnp.dot(own_ds, own_k, preferred_element_type=jnp.float32)) * score_scale
    query_grad = query_grad.reshape(token_count, block_width, head_dim).astype(jnp.bfloat16)
    local_key = jnp.dot(own_ds.T, flat_query, preferred_element_type=jnp.float32) * score_scale
    local_value = jnp.dot(own_prob.astype(jnp.bfloat16).T, flat_grad, preferred_element_type=jnp.float32)
    cart_key = jnp.dot(cart_ds.T, flat_query, preferred_element_type=jnp.float32) * score_scale
    cart_value = jnp.dot(cart_prob.astype(jnp.bfloat16).T, flat_grad, preferred_element_type=jnp.float32)
    return query_grad, local_key, local_value, cart_key, cart_value


def reference(queries, out_grad, self_keys, self_values, cart_keys, cart_values, segment_ids):
    row_count, token_count = segment_ids.shape
    head_count, head_dim = queries.shape[1], queries.shape[2]
    kv_count = cart_keys.shape[1]
    group_width = head_count // kv_count
    query_blocks = queries.reshape(row_count, token_count, kv_count, group_width, head_dim)
    grad_blocks = out_grad.reshape(row_count, token_count, kv_count, group_width, head_dim)
    key_blocks = self_keys.reshape(row_count, token_count, kv_count, head_dim)
    value_blocks = self_values.reshape(row_count, token_count, kv_count, head_dim)

    def one_row(running, inputs):
        query_row, grad_row, key_row, value_row, segment_row = inputs
        visible = block_masks(segment_row)

        def one_group(query_group, grad_group, cart_k, cart_v, own_k, own_v):
            return head_block(query_group, grad_group, visible, cart_k, cart_v, own_k, own_v)

        query_grad, local_key, local_value, cart_key, cart_value = jax.vmap(one_group, in_axes=1)(query_row, grad_row, cart_keys, cart_values, key_row, value_row)
        running = running + jnp.stack([cart_key, cart_value], axis=0).transpose(2, 0, 1, 3)
        query_flat = query_grad.transpose(1, 0, 2, 3).reshape(token_count, head_count * head_dim)
        local_pair = jnp.stack([local_key, local_value], axis=0).transpose(0, 2, 1, 3).astype(jnp.bfloat16)
        return running, (query_flat, local_pair)

    start_sum = jnp.zeros((cart_keys.shape[0], 2, kv_count, head_dim), jnp.float32)
    cart_grads, (query_rows, local_pairs) = lax.scan(one_row, start_sum, (query_blocks, grad_blocks, key_blocks, value_blocks, segment_ids))
    query_grads = query_rows.reshape(row_count * token_count, head_count * head_dim)
    self_grads = local_pairs.transpose(1, 0, 2, 3, 4).reshape(2, row_count * token_count, kv_count, head_dim)
    return cart_grads, self_grads, query_grads
```

```python
import functools
import math

import jax
import jax.numpy as jnp
from jax import lax
from jax.experimental import pallas as pl
from jax.experimental.pallas import tpu as pltpu
from jax.sharding import PartitionSpec as P

F32 = jnp.float32
BF16 = jnp.bfloat16
MASKED = -1e30
MESH = pl.DeviceIdType.MESH


def nt(a, b):
    return lax.dot_general(a, b, (((1,), (1,)), ((), ())), preferred_element_type=F32)


def tn(a, b):
    return lax.dot_general(a, b, (((0,), (0,)), ((), ())), preferred_element_type=F32)


def kernel(
    ndp, nh,
    seg_col, seg_row, q_ref, g_ref, k_ref, v_ref,
    dq_out, cart_out, self_out,
    bias, p_scr, ds_scr, dq_buf, stage, land,
    dq_send, dq_recv, dq_loc, rs_send, rs_recv,
):
    heads, tok, dim = q_ref.shape
    kvs, keys, _ = k_ref.shape
    cart = keys - tok
    width = heads // kvs
    share = cart // ndp
    piece = tok // nh
    scale = dim ** -0.5
    expo = scale * math.log2(math.e)
    my_dp = lax.axis_index("dp")
    my_h = lax.axis_index("heads")

    barrier = pltpu.get_barrier_semaphore()

    def greet_dp(i, c):
        pl.semaphore_signal(barrier, inc=1, device_id={"dp": lax.rem(my_dp + i, ndp)}, device_id_type=MESH)
        return c

    def greet_h(i, c):
        pl.semaphore_signal(barrier, inc=1, device_id={"heads": lax.rem(my_h + i, nh)}, device_id_type=MESH)
        return c

    lax.fori_loop(1, ndp, greet_dp, 0)
    lax.fori_loop(1, nh, greet_h, 0)
    pl.semaphore_wait(barrier, ndp - 1 + nh - 1)

    u_pos = lax.broadcasted_iota(jnp.int32, (tok, tok), 0)
    t_pos = lax.broadcasted_iota(jnp.int32, (tok, tok), 1)
    seen = (seg_col[...] == seg_row[...]) & (u_pos <= t_pos)
    bias[...] = jnp.where(seen, 0.0, MASKED)

    def dq_copy(kv, i):
        to = lax.rem(my_h + i, nh)
        cols = width * dim
        return pltpu.make_async_remote_copy(
            src_ref=dq_buf.at[pl.ds(pl.multiple_of(to * piece, piece), piece), pl.ds(kv * cols, cols)],
            dst_ref=dq_out.at[:, pl.ds(pl.multiple_of(my_h * heads * dim + kv * cols, cols), cols)],
            send_sem=dq_send.at[kv, i - 1],
            recv_sem=dq_recv.at[kv, i - 1],
            device_id={"heads": to},
            device_id_type=MESH,
        )

    def dq_arrival(kv, i):
        source = lax.rem(my_h - i + nh, nh)
        cols = width * dim
        landed = dq_out.at[:, pl.ds(pl.multiple_of(source * heads * dim + kv * cols, cols), cols)]
        return pltpu.make_async_remote_copy(
            src_ref=landed, dst_ref=landed,
            send_sem=dq_send.at[kv, i - 1],
            recv_sem=dq_recv.at[kv, i - 1],
            device_id={"heads": source},
            device_id_type=MESH,
        )

    def dq_own(kv):
        cols = width * dim
        return pltpu.make_async_copy(
            dq_buf.at[pl.ds(pl.multiple_of(my_h * piece, piece), piece), pl.ds(kv * cols, cols)],
            dq_out.at[:, pl.ds(pl.multiple_of(my_h * heads * dim + kv * cols, cols), cols)],
            dq_loc.at[kv],
        )

    def rs_copy(kv, i):
        return pltpu.make_async_remote_copy(
            src_ref=stage.at[kv, i - 1],
            dst_ref=land.at[kv, i - 1],
            send_sem=rs_send.at[kv, i - 1],
            recv_sem=rs_recv.at[kv, i - 1],
            device_id={"dp": lax.rem(my_dp + i, ndp)},
            device_id_type=MESH,
        )

    for kv in range(kvs):
        def one_head(j, c, kv=kv):
            h = kv * width + j
            qh = q_ref[h]
            gh = g_ref[h]
            s = nt(k_ref[kv], qh)
            s_cart = s[:cart]
            s_own = s[cart:] + bias[...]
            peak = jnp.maximum(
                jnp.max(s_cart, axis=0, keepdims=True), jnp.max(s_own, axis=0, keepdims=True)
            )
            e_cart = jnp.exp2((s_cart - peak) * expo)
            e_own = jnp.exp2((s_own - peak) * expo)
            total = jnp.sum(e_cart, axis=0, keepdims=True) + jnp.sum(e_own, axis=0, keepdims=True)
            dp = nt(v_ref[kv], gh)
            inverse = 1.0 / total
            center = (
                jnp.sum(e_cart * dp[:cart], axis=0, keepdims=True)
                + jnp.sum(e_own * dp[cart:], axis=0, keepdims=True)
            ) * inverse
            at = pl.ds(pl.multiple_of(j * tok, tok), tok)
            p_cart = e_cart * inverse
            p_own = e_own * inverse
            p_scr[:cart, at] = p_cart.astype(BF16)
            p_scr[cart:, at] = p_own.astype(BF16)
            ds_cart = (p_cart * (dp[:cart] - center)).astype(BF16)
            ds_own = (p_own * (dp[cart:] - center)).astype(BF16)
            ds_scr[:cart, at] = ds_cart
            ds_scr[cart:, at] = ds_own
            dq = tn(ds_scr[:, at], k_ref[kv]) * scale
            dq_buf[:, pl.ds(pl.multiple_of(h * dim, dim), dim)] = dq.astype(BF16)
            return c

        lax.fori_loop(0, width, one_head, 0)

        dq_own(kv).start()

        def send_dq(i, c, kv=kv):
            dq_copy(kv, i).start()
            return c

        lax.fori_loop(1, nh, send_dq, 0)

        q_rows = q_ref[kv * width : (kv + 1) * width].reshape(width * tok, dim)
        g_rows = g_ref[kv * width : (kv + 1) * width].reshape(width * tok, dim)

        def key_block(rows):
            dk = jnp.dot(ds_scr[rows, :], q_rows, preferred_element_type=F32) * scale
            dv = jnp.dot(p_scr[rows, :], g_rows, preferred_element_type=F32)
            return dk, dv

        def send_share(i, c, kv=kv, key_block=key_block):
            to = lax.rem(my_dp + i, ndp)
            dk, dv = key_block(pl.ds(pl.multiple_of(to * share, share), share))
            stage[kv, i - 1, 0] = dk.astype(BF16)
            stage[kv, i - 1, 1] = dv.astype(BF16)
            rs_copy(kv, i).start()
            return c

        lax.fori_loop(1, ndp, send_share, 0)
        dk, dv = key_block(pl.ds(pl.multiple_of(my_dp * share, share), share))
        cart_out[kv, 0] = dk
        cart_out[kv, 1] = dv
        dk, dv = key_block(pl.ds(cart, tok))
        self_out[0, kv] = dk.astype(BF16)
        self_out[1, kv] = dv.astype(BF16)

    for kv in range(kvs):
        dq_own(kv).wait()

        def end_dq(i, c, kv=kv):
            dq_copy(kv, i).wait_send()
            dq_arrival(kv, i).wait_recv()
            return c

        lax.fori_loop(1, nh, end_dq, 0)

        def end_rs(i, c, kv=kv):
            rs_copy(kv, i).wait_send()
            rs_copy(kv, i).wait_recv()
            cart_out[kv] += land[kv, i - 1].astype(F32)
            return c

        lax.fori_loop(1, ndp, end_rs, 0)


def on_device(ndp, nh, queries, out_grad, self_keys, self_values, cart_keys, cart_values, segment_ids):
    tok, heads, dim = queries.shape
    kvs = self_keys.shape[1]
    cart = cart_keys.shape[0]
    keys = cart + tok
    width = heads // kvs
    share = cart // ndp
    piece = tok // nh
    q = queries.transpose(1, 0, 2)
    g = out_grad.transpose(1, 0, 2)
    k = jnp.concatenate([cart_keys, self_keys], axis=0).transpose(1, 0, 2)
    v = jnp.concatenate([cart_values, self_values], axis=0).transpose(1, 0, 2)
    vmem = pl.BlockSpec(memory_space=pltpu.VMEM)
    dma = pltpu.SemaphoreType.DMA
    query_grads, cart_part, self_part = pl.pallas_call(
        functools.partial(kernel, ndp, nh),
        out_shape=(
            jax.ShapeDtypeStruct((piece, nh * heads * dim), BF16),
            jax.ShapeDtypeStruct((kvs, 2, share, dim), F32),
            jax.ShapeDtypeStruct((2, kvs, tok, dim), BF16),
        ),
        in_specs=[vmem] * 6,
        out_specs=(pl.BlockSpec(memory_space=pl.ANY), vmem, vmem),
        scratch_shapes=[
            pltpu.VMEM((tok, tok), F32),
            pltpu.VMEM((keys, width * tok), BF16),
            pltpu.VMEM((keys, width * tok), BF16),
            pltpu.VMEM((tok, heads * dim), BF16),
            pltpu.VMEM((kvs, ndp - 1, 2, share, dim), BF16),
            pltpu.VMEM((kvs, ndp - 1, 2, share, dim), BF16),
            dma((kvs, nh - 1)),
            dma((kvs, nh - 1)),
            dma((kvs,)),
            dma((kvs, ndp - 1)),
            dma((kvs, ndp - 1)),
        ],
        compiler_params=pltpu.CompilerParams(
            collective_id=0, has_side_effects=True, vmem_limit_bytes=60 << 20
        ),
        name="attention_backward",
    )(segment_ids.reshape(tok, 1), segment_ids.reshape(1, tok), q, g, k, v)
    cart_grads = cart_part.transpose(2, 1, 0, 3)
    self_grads = self_part.transpose(0, 2, 1, 3)
    return cart_grads, self_grads, query_grads


def solution(mesh):
    in_specs = (
        P(("groups", "dp"), "heads", None),
        P(("groups", "dp"), "heads", None),
        P(("groups", "dp"), "heads", None),
        P(("groups", "dp"), "heads", None),
        P("groups", "heads", None),
        P("groups", "heads", None),
        P(("groups", "dp"), None),
    )
    out_specs = (
        P(("groups", "dp"), None, "heads", None),
        P(None, ("groups", "dp"), "heads", None),
        P(("groups", "dp", "heads"), None),
    )
    body = functools.partial(on_device, mesh.shape["dp"], mesh.shape["heads"])
    return jax.shard_map(body, mesh=mesh, in_specs=in_specs, out_specs=out_specs, check_vma=False)
```

```python
import functools
import math

import jax
import jax.numpy as jnp
from jax import lax
from jax.experimental import pallas as pl
from jax.experimental.pallas import tpu as pltpu
from jax.sharding import PartitionSpec as P

F32 = jnp.float32
BF16 = jnp.bfloat16
MASKED = -1e30
MESH = pl.DeviceIdType.MESH


def nt(a, b):
    return lax.dot_general(a, b, (((1,), (1,)), ((), ())), preferred_element_type=F32)


def tn(a, b):
    return lax.dot_general(a, b, (((0,), (0,)), ((), ())), preferred_element_type=F32)


def kernel(
    ndp, nh, kvs,
    seg_ref, q_ref, g_ref, ck_ref, cv_ref, sk_ref, sv_ref,
    dq_out, cart_out, self_out,
    bias, k_scr, v_scr, wide, s_a, d_a, m_a, w_a, s_b, d_b, m_b, w_b,
    p_scr, ds_scr, dq_buf, stage, land, cart_acc, self_acc,
    dq_send, dq_recv, dq_loc, rs_send, rs_recv,
):
    tok, heads, dim = q_ref.shape
    cart = ck_ref.shape[0] // kvs
    keys = cart + tok
    width = heads // kvs
    share = cart // ndp
    piece = tok // nh
    step = s_a.shape[1]
    span = step // width
    blocks = tok // span
    chunk = 128
    scale = dim ** -0.5
    expo = scale * math.log2(math.e)
    my_dp = lax.axis_index("dp")
    my_h = lax.axis_index("heads")

    barrier = pltpu.get_barrier_semaphore()

    def greet_dp(i, c):
        pl.semaphore_signal(barrier, inc=1, device_id={"dp": lax.rem(my_dp + i, ndp)}, device_id_type=MESH)
        return c

    def greet_h(i, c):
        pl.semaphore_signal(barrier, inc=1, device_id={"heads": lax.rem(my_h + i, nh)}, device_id_type=MESH)
        return c

    lax.fori_loop(1, ndp, greet_dp, 0)
    lax.fori_loop(1, nh, greet_h, 0)

    def split_heads(src, dst, base):
        rows = src.shape[0] // kvs
        if kvs == 1:
            dst[0, pl.ds(base, rows)] = src[...]
            return
        wide[: rows * kvs] = src[...].astype(F32)
        for kv in range(kvs):
            dst[kv, pl.ds(base, rows)] = wide[pl.ds(kv, rows, stride=kvs)].astype(BF16)

    split_heads(ck_ref, k_scr, 0)
    split_heads(sk_ref, k_scr, cart)
    split_heads(cv_ref, v_scr, 0)
    split_heads(sv_ref, v_scr, cart)

    seg_u = jnp.broadcast_to(seg_ref[...], (tok, tok))
    seg_t = seg_u.T
    t_pos = lax.broadcasted_iota(jnp.int32, (tok, tok), 0)
    u_pos = lax.broadcasted_iota(jnp.int32, (tok, tok), 1)
    seen = jnp.where((seg_u == seg_t) & (u_pos <= t_pos), 1.0, 0.0).astype(BF16)
    spread = jnp.where(
        lax.broadcasted_iota(jnp.int32, (span, step), 1) // width
        == lax.broadcasted_iota(jnp.int32, (span, step), 0),
        1.0, 0.0,
    ).astype(BF16)
    for b in range(blocks):
        bias[b] = (tn(seen[b * span : (b + 1) * span], spread) - 1.0) * -MASKED

    def rows_of(ref, kv, b):
        heads_at = pl.ds(pl.multiple_of(kv * width, width), width)
        return ref[pl.ds(b * span, span), heads_at, :].reshape(step, dim)

    def score(kv, b, s_x, d_x, m_x):
        qb = rows_of(q_ref, kv, b)
        gb = rows_of(g_ref, kv, b)
        peak = None
        for lo in range(0, keys, chunk):
            s = nt(k_scr[kv, lo : lo + chunk], qb)
            if lo >= cart:
                s = s + bias[b, lo - cart : lo - cart + chunk]
            s_x[lo : lo + chunk] = s
            top = jnp.max(s.reshape(chunk // 8, 8, step), axis=0)
            peak = top if peak is None else jnp.maximum(peak, top)
            d_x[lo : lo + chunk] = nt(v_scr[kv, lo : lo + chunk], gb)
        m_x[...] = jnp.broadcast_to(jnp.max(peak, axis=0, keepdims=True), (8, step))

    def backward(kv, b, s_x, d_x, m_x, w_x):
        peak = m_x[:1]
        total = jnp.zeros((8, step), F32)
        mixed = jnp.zeros((8, step), F32)
        for lo in range(0, keys, chunk):
            e = jnp.exp2((s_x[lo : lo + chunk] - peak) * expo)
            s_x[lo : lo + chunk] = e
            total = total + jnp.sum(e.reshape(chunk // 8, 8, step), axis=0)
            ed = e * d_x[lo : lo + chunk]
            mixed = mixed + jnp.sum(ed.reshape(chunk // 8, 8, step), axis=0)
        inverse = 1.0 / jnp.sum(total, axis=0, keepdims=True)
        center = jnp.sum(mixed, axis=0, keepdims=True) * inverse
        at = pl.ds(pl.multiple_of(b * step, step), step)
        for lo in range(0, keys, chunk):
            p = s_x[lo : lo + chunk] * inverse
            p_scr[lo : lo + chunk, at] = p.astype(BF16)
            ds_scr[lo : lo + chunk, at] = (p * (d_x[lo : lo + chunk] - center)).astype(BF16)
        w_x[...] = tn(ds_scr[:, at], k_scr[kv]) * scale
        rows = pl.ds(pl.multiple_of(b * span, span), span)
        for hh in range(width):
            out = w_x[pl.ds(hh, span, stride=width)].astype(BF16)
            dq_buf[rows, kv * cols + hh * dim : kv * cols + (hh + 1) * dim] = out

    cols = width * dim

    def dq_copy(kv, i):
        to = lax.rem(my_h + i, nh)
        return pltpu.make_async_remote_copy(
            src_ref=dq_buf.at[pl.ds(pl.multiple_of(to * piece, piece), piece), pl.ds(kv * cols, cols)],
            dst_ref=dq_out.at[:, pl.ds(pl.multiple_of(my_h * heads * dim + kv * cols, cols), cols)],
            send_sem=dq_send.at[kv, i - 1],
            recv_sem=dq_recv.at[kv, i - 1],
            device_id={"heads": to},
            device_id_type=MESH,
        )

    def dq_arrival(kv, i):
        source = lax.rem(my_h - i + nh, nh)
        landed = dq_out.at[:, pl.ds(pl.multiple_of(source * heads * dim + kv * cols, cols), cols)]
        return pltpu.make_async_remote_copy(
            src_ref=landed, dst_ref=landed,
            send_sem=dq_send.at[kv, i - 1],
            recv_sem=dq_recv.at[kv, i - 1],
            device_id={"heads": source},
            device_id_type=MESH,
        )

    def dq_own(kv):
        return pltpu.make_async_copy(
            dq_buf.at[pl.ds(pl.multiple_of(my_h * piece, piece), piece), pl.ds(kv * cols, cols)],
            dq_out.at[:, pl.ds(pl.multiple_of(my_h * heads * dim + kv * cols, cols), cols)],
            dq_loc.at[kv],
        )

    def rs_copy(kv, i):
        return pltpu.make_async_remote_copy(
            src_ref=stage.at[kv, i - 1],
            dst_ref=land.at[kv, i - 1],
            send_sem=rs_send.at[kv, i - 1],
            recv_sem=rs_recv.at[kv, i - 1],
            device_id={"dp": lax.rem(my_dp + i, ndp)},
            device_id_type=MESH,
        )

    score(0, 0, s_a, d_a, m_a)
    pl.semaphore_wait(barrier, ndp - 1 + nh - 1)

    for kv in range(kvs):
        def two_blocks(i, c, kv=kv):
            score(kv, 2 * i + 1, s_b, d_b, m_b)
            backward(kv, 2 * i, s_a, d_a, m_a, w_a)
            after = kv * blocks + 2 * i + 2
            score(jnp.minimum(after // blocks, kvs - 1), lax.rem(after, blocks), s_a, d_a, m_a)
            backward(kv, 2 * i + 1, s_b, d_b, m_b, w_b)
            return c

        lax.fori_loop(0, blocks // 2, two_blocks, 0)

        dq_own(kv).start()

        def send_dq(i, c, kv=kv):
            dq_copy(kv, i).start()
            return c

        lax.fori_loop(1, nh, send_dq, 0)

        q_rows = q_ref[:, kv * width : (kv + 1) * width, :].reshape(width * tok, dim)
        g_rows = g_ref[:, kv * width : (kv + 1) * width, :].reshape(width * tok, dim)

        def key_block(rows):
            dk = jnp.dot(ds_scr[rows, :], q_rows, preferred_element_type=F32) * scale
            dv = jnp.dot(p_scr[rows, :], g_rows, preferred_element_type=F32)
            return dk, dv

        def send_share(i, c, kv=kv, key_block=key_block):
            to = lax.rem(my_dp + i, ndp)
            dk, dv = key_block(pl.ds(pl.multiple_of(to * share, share), share))
            stage[kv, i - 1, 0] = dk.astype(BF16)
            stage[kv, i - 1, 1] = dv.astype(BF16)
            rs_copy(kv, i).start()
            return c

        lax.fori_loop(1, ndp, send_share, 0)
        dk, dv = key_block(pl.ds(pl.multiple_of(my_dp * share, share), share))
        cart_acc[kv, 0] = dk
        cart_acc[kv, 1] = dv
        dk, dv = key_block(pl.ds(cart, tok))
        self_acc[pl.ds(kv, tok, stride=kvs)] = dk
        self_acc[pl.ds(tok * kvs + kv, tok, stride=kvs)] = dv

    self_out[...] = self_acc[...].astype(BF16)

    for kv in range(kvs):
        dq_own(kv).wait()

        def end_dq(i, c, kv=kv):
            dq_copy(kv, i).wait_send()
            dq_arrival(kv, i).wait_recv()
            return c

        lax.fori_loop(1, nh, end_dq, 0)

        def end_rs(i, c, kv=kv):
            rs_copy(kv, i).wait_send()
            rs_copy(kv, i).wait_recv()
            cart_acc[kv] += land[kv, i - 1].astype(F32)
            return c

        lax.fori_loop(1, ndp, end_rs, 0)
        for kind in range(2):
            cart_out[pl.ds(kind * kvs + kv, share, stride=2 * kvs)] = cart_acc[kv, kind]


def on_device(ndp, nh, queries, out_grad, self_keys, self_values, cart_keys, cart_values, segment_ids):
    tok, heads, dim = queries.shape
    kvs = self_keys.shape[1]
    cart = cart_keys.shape[0]
    keys = cart + tok
    width = heads // kvs
    share = cart // ndp
    piece = tok // nh
    step = 256
    vmem = pl.BlockSpec(memory_space=pltpu.VMEM)
    dma = pltpu.SemaphoreType.DMA
    query_grads, cart_part, self_part = pl.pallas_call(
        functools.partial(kernel, ndp, nh, kvs),
        out_shape=(
            jax.ShapeDtypeStruct((piece, nh * heads * dim), BF16),
            jax.ShapeDtypeStruct((share * 2 * kvs, dim), F32),
            jax.ShapeDtypeStruct((2 * tok * kvs, dim), BF16),
        ),
        in_specs=[vmem] * 7,
        out_specs=(pl.BlockSpec(memory_space=pl.ANY), vmem, vmem),
        scratch_shapes=[
            pltpu.VMEM((tok * width // step, tok, step), F32),
            pltpu.VMEM((kvs, keys, dim), BF16),
            pltpu.VMEM((kvs, keys, dim), BF16),
            pltpu.VMEM((cart * kvs, dim), F32),
            pltpu.VMEM((keys, step), F32),
            pltpu.VMEM((keys, step), F32),
            pltpu.VMEM((8, step), F32),
            pltpu.VMEM((step, dim), F32),
            pltpu.VMEM((keys, step), F32),
            pltpu.VMEM((keys, step), F32),
            pltpu.VMEM((8, step), F32),
            pltpu.VMEM((step, dim), F32),
            pltpu.VMEM((keys, width * tok), BF16),
            pltpu.VMEM((keys, width * tok), BF16),
            pltpu.VMEM((tok, heads * dim), BF16),
            pltpu.VMEM((kvs, ndp - 1, 2, share, dim), BF16),
            pltpu.VMEM((kvs, ndp - 1, 2, share, dim), BF16),
            pltpu.VMEM((kvs, 2, share, dim), F32),
            pltpu.VMEM((2 * tok * kvs, dim), F32),
            dma((kvs, nh - 1)),
            dma((kvs, nh - 1)),
            dma((kvs,)),
            dma((kvs, ndp - 1)),
            dma((kvs, ndp - 1)),
        ],
        compiler_params=pltpu.CompilerParams(
            collective_id=0, has_side_effects=True, vmem_limit_bytes=60 << 20
        ),
        name="attention_backward",
    )(
        segment_ids, queries, out_grad,
        cart_keys.reshape(cart * kvs, dim), cart_values.reshape(cart * kvs, dim),
        self_keys.reshape(tok * kvs, dim), self_values.reshape(tok * kvs, dim),
    )
    cart_grads = cart_part.reshape(share, 2, kvs, dim)
    self_grads = self_part.reshape(2, tok, kvs, dim)
    return cart_grads, self_grads, query_grads


def solution(mesh):
    in_specs = (
        P(("groups", "dp"), "heads", None),
        P(("groups", "dp"), "heads", None),
        P(("groups", "dp"), "heads", None),
        P(("groups", "dp"), "heads", None),
        P("groups", "heads", None),
        P("groups", "heads", None),
        P(("groups", "dp"), None),
    )
    out_specs = (
        P(("groups", "dp"), None, "heads", None),
        P(None, ("groups", "dp"), "heads", None),
        P(("groups", "dp", "heads"), None),
    )
    body = functools.partial(on_device, mesh.shape["dp"], mesh.shape["heads"])
    return jax.shard_map(body, mesh=mesh, in_specs=in_specs, out_specs=out_specs, check_vma=False)
```

```python
import functools
import math

import jax
import jax.numpy as jnp
from jax import lax
from jax.experimental import pallas as pl
from jax.experimental.pallas import tpu as pltpu
from jax.sharding import PartitionSpec as P

F32 = jnp.float32
BF16 = jnp.bfloat16
MASKED = -1e30
CHUNK = 256
FINE = 64
MESH = pl.DeviceIdType.MESH


def nt(a, b):
    return lax.dot_general(a, b, (((1,), (1,)), ((), ())), preferred_element_type=F32)


def tn(a, b):
    return lax.dot_general(a, b, (((0,), (0,)), ((), ())), preferred_element_type=F32)


def kernel(
    ndp, nh, kvs,
    seg_ref, q_ref, g_ref, ck_ref, cv_ref, sk_ref, sv_ref,
    dq_out, cart_out, self_out,
    bias, k_scr, v_scr, wide, s_a, d_a, m_a, w_a, s_b, d_b, m_b, w_b,
    p_scr, ds_scr, dq_buf, stage, land, cart_acc, self_acc,
    dq_send, dq_recv, dq_loc, rs_send, rs_recv,
):
    tok, heads, dim = q_ref.shape
    cart = ck_ref.shape[0] // kvs
    keys = cart + tok
    width = heads // kvs
    share = cart // ndp
    piece = tok // nh
    step = s_a.shape[1]
    span = step // width
    blocks = tok // span
    chunk = CHUNK
    fine = FINE
    scale = dim ** -0.5
    expo = scale * math.log2(math.e)
    my_dp = lax.axis_index("dp")
    my_h = lax.axis_index("heads")

    barrier = pltpu.get_barrier_semaphore()

    def greet_dp(i, c):
        pl.semaphore_signal(barrier, inc=1, device_id={"dp": lax.rem(my_dp + i, ndp)}, device_id_type=MESH)
        return c

    def greet_h(i, c):
        pl.semaphore_signal(barrier, inc=1, device_id={"heads": lax.rem(my_h + i, nh)}, device_id_type=MESH)
        return c

    lax.fori_loop(1, ndp, greet_dp, 0)
    lax.fori_loop(1, nh, greet_h, 0)

    def split_heads(src, dst, base):
        rows = src.shape[0] // kvs
        if kvs == 1:
            dst[0, pl.ds(base, rows)] = src[...]
            return
        wide[: rows * kvs] = src[...].astype(F32)
        for kv in range(kvs):
            dst[kv, pl.ds(base, rows)] = wide[pl.ds(kv, rows, stride=kvs)].astype(BF16)

    split_heads(ck_ref, k_scr, 0)
    split_heads(sk_ref, k_scr, cart)
    split_heads(cv_ref, v_scr, 0)
    split_heads(sv_ref, v_scr, cart)

    seg_u = jnp.broadcast_to(seg_ref[...], (tok, tok))
    seg_t = seg_u.T
    t_pos = lax.broadcasted_iota(jnp.int32, (tok, tok), 0)
    u_pos = lax.broadcasted_iota(jnp.int32, (tok, tok), 1)
    seen = jnp.where((seg_u == seg_t) & (u_pos <= t_pos), 1.0, 0.0).astype(BF16)
    spread = jnp.where(
        lax.broadcasted_iota(jnp.int32, (span, step), 1) // width
        == lax.broadcasted_iota(jnp.int32, (span, step), 0),
        1.0, 0.0,
    ).astype(BF16)
    for b in range(blocks):
        bias[b] = (tn(seen[b * span : (b + 1) * span], spread) - 1.0) * -MASKED

    def rows_of(ref, kv, b):
        heads_at = pl.ds(pl.multiple_of(kv * width, width), width)
        return ref[pl.ds(b * span, span), heads_at, :].reshape(step, dim)

    def score_chunk(kv, b, lo, qb, gb, s_x, d_x, peak):
        s = nt(k_scr[kv, lo : lo + chunk], qb)
        if lo >= cart:
            s = s + bias[b, lo - cart : lo - cart + chunk]
        s_x[lo : lo + chunk] = s
        top = jnp.max(s.reshape(chunk // 8, 8, step), axis=0)
        d_x[lo : lo + chunk] = nt(v_scr[kv, lo : lo + chunk], gb)
        return top if peak is None else jnp.maximum(peak, top)

    def settle(peak, m_x):
        m_x[...] = jnp.broadcast_to(jnp.max(peak, axis=0, keepdims=True), (8, step))

    def score(kv, b, s_x, d_x, m_x):
        qb = rows_of(q_ref, kv, b)
        gb = rows_of(g_ref, kv, b)
        peak = None
        for lo in range(0, keys, chunk):
            peak = score_chunk(kv, b, lo, qb, gb, s_x, d_x, peak)
        settle(peak, m_x)

    def score_and_backward(kv_s, b_s, s_y, d_y, m_y, kv, b, s_x, d_x, m_x, w_x):
        qb = rows_of(q_ref, kv_s, b_s)
        gb = rows_of(g_ref, kv_s, b_s)
        peak_y = None
        peak = m_x[:1]
        total = jnp.zeros((8, step), F32)
        mixed = jnp.zeros((8, step), F32)
        for lo in range(0, keys, chunk):
            peak_y = score_chunk(kv_s, b_s, lo, qb, gb, s_y, d_y, peak_y)
            for at in range(lo, lo + chunk, fine):
                e = jnp.exp2((s_x[at : at + fine] - peak) * expo)
                s_x[at : at + fine] = e
                total = total + jnp.sum(e.reshape(fine // 8, 8, step), axis=0)
                ed = e * d_x[at : at + fine]
                mixed = mixed + jnp.sum(ed.reshape(fine // 8, 8, step), axis=0)
        settle(peak_y, m_y)
        inverse = 1.0 / jnp.sum(total, axis=0, keepdims=True)
        center = jnp.sum(mixed, axis=0, keepdims=True) * inverse
        here = pl.ds(pl.multiple_of(b * step, step), step)
        dq = None
        for lo in range(0, keys, 256):
            for at in range(lo, lo + 256, fine):
                p = s_x[at : at + fine] * inverse
                p_scr[at : at + fine, here] = p.astype(BF16)
                ds_scr[at : at + fine, here] = (p * (d_x[at : at + fine] - center)).astype(BF16)
            part = tn(ds_scr[lo : lo + 256, here], k_scr[kv, lo : lo + 256])
            dq = part if dq is None else dq + part
        w_x[...] = dq * scale
        rows = pl.ds(pl.multiple_of(b * span, span), span)
        for hh in range(width):
            out = w_x[pl.ds(hh, span, stride=width)].astype(BF16)
            dq_buf[rows, kv * cols + hh * dim : kv * cols + (hh + 1) * dim] = out

    cols = width * dim
    done = 2 * span // piece

    def dq_copy(kv, i):
        to = lax.rem(my_h + i, nh)
        return pltpu.make_async_remote_copy(
            src_ref=dq_buf.at[pl.ds(pl.multiple_of(to * piece, piece), piece), pl.ds(kv * cols, cols)],
            dst_ref=dq_out.at[:, pl.ds(pl.multiple_of(my_h * heads * dim + kv * cols, cols), cols)],
            send_sem=dq_send.at[kv, i - 1],
            recv_sem=dq_recv.at[kv, i - 1],
            device_id={"heads": to},
            device_id_type=MESH,
        )

    def dq_arrival(kv, i):
        source = lax.rem(my_h - i + nh, nh)
        landed = dq_out.at[:, pl.ds(pl.multiple_of(source * heads * dim + kv * cols, cols), cols)]
        return pltpu.make_async_remote_copy(
            src_ref=landed, dst_ref=landed,
            send_sem=dq_send.at[kv, i - 1],
            recv_sem=dq_recv.at[kv, i - 1],
            device_id={"heads": source},
            device_id_type=MESH,
        )

    def dq_own(kv):
        return pltpu.make_async_copy(
            dq_buf.at[pl.ds(pl.multiple_of(my_h * piece, piece), piece), pl.ds(kv * cols, cols)],
            dq_out.at[:, pl.ds(pl.multiple_of(my_h * heads * dim + kv * cols, cols), cols)],
            dq_loc.at[kv],
        )

    def rs_copy(kv, i):
        return pltpu.make_async_remote_copy(
            src_ref=stage.at[kv, i - 1],
            dst_ref=land.at[kv, i - 1],
            send_sem=rs_send.at[kv, i - 1],
            recv_sem=rs_recv.at[kv, i - 1],
            device_id={"dp": lax.rem(my_dp + i, ndp)},
            device_id_type=MESH,
        )

    score(0, 0, s_a, d_a, m_a)
    pl.semaphore_wait(barrier, ndp - 1 + nh - 1)

    for kv in range(kvs):
        def two_blocks(i, c, kv=kv):
            score_and_backward(
                kv, 2 * i + 1, s_b, d_b, m_b,
                kv, 2 * i, s_a, d_a, m_a, w_a,
            )
            after = kv * blocks + 2 * i + 2
            score_and_backward(
                jnp.minimum(after // blocks, kvs - 1), lax.rem(after, blocks), s_a, d_a, m_a,
                kv, 2 * i + 1, s_b, d_b, m_b, w_b,
            )
            for t in range(done):
                away = lax.rem(i * done + t - my_h + nh, nh)

                @pl.when(away == 0)
                def _():
                    dq_own(kv).start()

                @pl.when(away != 0)
                def _():
                    dq_copy(kv, away).start()

            return c

        lax.fori_loop(0, blocks // 2, two_blocks, 0)

        q_rows = q_ref[:, kv * width : (kv + 1) * width, :].reshape(width * tok, dim)
        g_rows = g_ref[:, kv * width : (kv + 1) * width, :].reshape(width * tok, dim)

        def key_block(rows):
            dk = jnp.dot(ds_scr[rows, :], q_rows, preferred_element_type=F32) * scale
            dv = jnp.dot(p_scr[rows, :], g_rows, preferred_element_type=F32)
            return dk, dv

        def send_share(i, c, kv=kv, key_block=key_block):
            to = lax.rem(my_dp + i, ndp)
            dk, dv = key_block(pl.ds(pl.multiple_of(to * share, share), share))
            stage[kv, i - 1, 0] = dk.astype(BF16)
            stage[kv, i - 1, 1] = dv.astype(BF16)
            rs_copy(kv, i).start()
            return c

        lax.fori_loop(1, ndp, send_share, 0)
        dk, dv = key_block(pl.ds(pl.multiple_of(my_dp * share, share), share))
        cart_acc[kv, 0] = dk
        cart_acc[kv, 1] = dv
        dk, dv = key_block(pl.ds(cart, tok))
        self_acc[pl.ds(kv, tok, stride=kvs)] = dk
        self_acc[pl.ds(tok * kvs + kv, tok, stride=kvs)] = dv

    self_out[...] = self_acc[...].astype(BF16)

    for kv in range(kvs):
        dq_own(kv).wait()

        def end_dq(i, c, kv=kv):
            dq_copy(kv, i).wait_send()
            dq_arrival(kv, i).wait_recv()
            return c

        lax.fori_loop(1, nh, end_dq, 0)

        def end_rs(i, c, kv=kv):
            rs_copy(kv, i).wait_send()
            rs_copy(kv, i).wait_recv()
            cart_acc[kv] += land[kv, i - 1].astype(F32)
            return c

        lax.fori_loop(1, ndp, end_rs, 0)
        for kind in range(2):
            cart_out[pl.ds(kind * kvs + kv, share, stride=2 * kvs)] = cart_acc[kv, kind]


def finish(dq_in, cart_in, self_in, dq_out, cart_out, self_out, dq_buf, cart_buf, self_buf, sems):
    trio = ((dq_in, dq_buf, dq_out), (cart_in, cart_buf, cart_out), (self_in, self_buf, self_out))
    for n, (src, buf, _) in enumerate(trio):
        pltpu.make_async_copy(src, buf, sems.at[0, n]).start()
    for n, (src, buf, dst) in enumerate(trio):
        pltpu.make_async_copy(src, buf, sems.at[0, n]).wait()
        pltpu.make_async_copy(buf, dst, sems.at[1, n]).start()
    for n, (_, buf, dst) in enumerate(trio):
        pltpu.make_async_copy(buf, dst, sems.at[1, n]).wait()


def on_device(ndp, nh, queries, out_grad, self_keys, self_values, cart_keys, cart_values, segment_ids):
    tok, heads, dim = queries.shape
    kvs = self_keys.shape[1]
    cart = cart_keys.shape[0]
    keys = cart + tok
    width = heads // kvs
    share = cart // ndp
    piece = tok // nh
    step = 256
    vmem = pl.BlockSpec(memory_space=pltpu.VMEM)
    dma = pltpu.SemaphoreType.DMA
    query_grads, cart_part, self_part = pl.pallas_call(
        functools.partial(kernel, ndp, nh, kvs),
        out_shape=(
            jax.ShapeDtypeStruct((piece, nh * heads * dim), BF16),
            jax.ShapeDtypeStruct((share * 2 * kvs, dim), F32),
            jax.ShapeDtypeStruct((2 * tok * kvs, dim), BF16),
        ),
        in_specs=[vmem] * 7,
        out_specs=(pl.BlockSpec(memory_space=pl.ANY), vmem, vmem),
        scratch_shapes=[
            pltpu.VMEM((tok * width // step, tok, step), F32),
            pltpu.VMEM((kvs, keys, dim), BF16),
            pltpu.VMEM((kvs, keys, dim), BF16),
            pltpu.VMEM((cart * kvs, dim), F32),
            pltpu.VMEM((keys, step), F32),
            pltpu.VMEM((keys, step), F32),
            pltpu.VMEM((8, step), F32),
            pltpu.VMEM((step, dim), F32),
            pltpu.VMEM((keys, step), F32),
            pltpu.VMEM((keys, step), F32),
            pltpu.VMEM((8, step), F32),
            pltpu.VMEM((step, dim), F32),
            pltpu.VMEM((keys, width * tok), BF16),
            pltpu.VMEM((keys, width * tok), BF16),
            pltpu.VMEM((tok, heads * dim), BF16),
            pltpu.VMEM((kvs, ndp - 1, 2, share, dim), BF16),
            pltpu.VMEM((kvs, ndp - 1, 2, share, dim), BF16),
            pltpu.VMEM((kvs, 2, share, dim), F32),
            pltpu.VMEM((2 * tok * kvs, dim), F32),
            dma((kvs, nh - 1)),
            dma((kvs, nh - 1)),
            dma((kvs,)),
            dma((kvs, ndp - 1)),
            dma((kvs, ndp - 1)),
        ],
        compiler_params=pltpu.CompilerParams(
            collective_id=0, has_side_effects=True, vmem_limit_bytes=60 << 20
        ),
        name="attention_backward",
    )(
        segment_ids, queries, out_grad,
        cart_keys.reshape(cart * kvs, dim), cart_values.reshape(cart * kvs, dim),
        self_keys.reshape(tok * kvs, dim), self_values.reshape(tok * kvs, dim),
    )
    parts = (query_grads, cart_part, self_part)
    anywhere = pl.BlockSpec(memory_space=pl.ANY)
    query_grads, cart_part, self_part = pl.pallas_call(
        finish,
        out_shape=tuple(jax.ShapeDtypeStruct(x.shape, x.dtype) for x in parts),
        in_specs=[anywhere] * 3,
        out_specs=(anywhere,) * 3,
        scratch_shapes=[pltpu.VMEM(x.shape, x.dtype) for x in parts] + [dma((2, 3))],
        name="finish",
    )(*parts)
    cart_grads = cart_part.reshape(share, 2, kvs, dim)
    self_grads = self_part.reshape(2, tok, kvs, dim)
    return cart_grads, self_grads, query_grads


def solution(mesh):
    in_specs = (
        P(("groups", "dp"), "heads", None),
        P(("groups", "dp"), "heads", None),
        P(("groups", "dp"), "heads", None),
        P(("groups", "dp"), "heads", None),
        P("groups", "heads", None),
        P("groups", "heads", None),
        P(("groups", "dp"), None),
    )
    out_specs = (
        P(("groups", "dp"), None, "heads", None),
        P(None, ("groups", "dp"), "heads", None),
        P(("groups", "dp", "heads"), None),
    )
    body = functools.partial(on_device, mesh.shape["dp"], mesh.shape["heads"])
    return jax.shard_map(body, mesh=mesh, in_specs=in_specs, out_specs=out_specs, check_vma=False)
```

```python
import functools
import math

import jax
import jax.numpy as jnp
from jax import lax
from jax.experimental import pallas as pl
from jax.experimental.pallas import tpu as pltpu
from jax.sharding import PartitionSpec as P

F32 = jnp.float32
BF16 = jnp.bfloat16
MASKED = -1e30
CHUNK = 128
FINE = 32
MESH = pl.DeviceIdType.MESH


def nt(a, b):
    return lax.dot_general(a, b, (((1,), (1,)), ((), ())), preferred_element_type=F32)


def tn(a, b):
    return lax.dot_general(a, b, (((0,), (0,)), ((), ())), preferred_element_type=F32)


def kernel(
    ndp, nh, kvs,
    seg_ref, q_ref, g_ref, ck_ref, cv_ref, sk_ref, sv_ref,
    dq_out, cart_out, self_out,
    bias, k_scr, v_scr, wide, s_a, d_a, m_a, w_a, s_b, d_b, m_b, w_b,
    p_scr, ds_scr, dq_buf, stage, land, cart_acc, self_acc,
    dq_send, dq_recv, dq_loc, rs_send, rs_recv,
):
    tok, heads, dim = q_ref.shape
    cart = ck_ref.shape[0] // kvs
    keys = cart + tok
    width = heads // kvs
    share = cart // ndp
    piece = tok // nh
    step = s_a.shape[1]
    span = step // width
    blocks = tok // span
    chunk = CHUNK
    fine = FINE
    scale = dim ** -0.5
    expo = scale * math.log2(math.e)
    my_dp = lax.axis_index("dp")
    my_h = lax.axis_index("heads")

    barrier = pltpu.get_barrier_semaphore()

    def greet_dp(i, c):
        pl.semaphore_signal(barrier, inc=1, device_id={"dp": lax.rem(my_dp + i, ndp)}, device_id_type=MESH)
        return c

    def greet_h(i, c):
        pl.semaphore_signal(barrier, inc=1, device_id={"heads": lax.rem(my_h + i, nh)}, device_id_type=MESH)
        return c

    lax.fori_loop(1, ndp, greet_dp, 0)
    lax.fori_loop(1, nh, greet_h, 0)

    def split_heads(src, dst, base):
        rows = src.shape[0] // kvs
        if kvs == 1:
            dst[0, pl.ds(base, rows)] = src[...]
            return
        wide[: rows * kvs] = src[...].astype(F32)
        for kv in range(kvs):
            dst[kv, pl.ds(base, rows)] = wide[pl.ds(kv, rows, stride=kvs)].astype(BF16)

    split_heads(ck_ref, k_scr, 0)
    split_heads(sk_ref, k_scr, cart)
    split_heads(cv_ref, v_scr, 0)
    split_heads(sv_ref, v_scr, cart)

    seg_u = jnp.broadcast_to(seg_ref[...], (tok, tok))
    seg_t = seg_u.T
    t_pos = lax.broadcasted_iota(jnp.int32, (tok, tok), 0)
    u_pos = lax.broadcasted_iota(jnp.int32, (tok, tok), 1)
    seen = jnp.where((seg_u == seg_t) & (u_pos <= t_pos), 1.0, 0.0).astype(BF16)
    spread = jnp.where(
        lax.broadcasted_iota(jnp.int32, (span, step), 1) // width
        == lax.broadcasted_iota(jnp.int32, (span, step), 0),
        1.0, 0.0,
    ).astype(BF16)
    for b in range(blocks):
        bias[b] = (tn(seen[b * span : (b + 1) * span], spread) - 1.0) * -MASKED

    def rows_of(ref, kv, b):
        heads_at = pl.ds(pl.multiple_of(kv * width, width), width)
        return ref[pl.ds(b * span, span), heads_at, :].reshape(step, dim)

    def score_chunk(kv, b, lo, qb, gb, s_x, d_x, peak):
        s = nt(k_scr[kv, lo : lo + chunk], qb)
        if lo >= cart:
            s = s + bias[b, lo - cart : lo - cart + chunk]
        s_x[lo : lo + chunk] = s
        top = jnp.max(s.reshape(chunk // 8, 8, step), axis=0)
        d_x[lo : lo + chunk] = nt(v_scr[kv, lo : lo + chunk], gb)
        return top if peak is None else jnp.maximum(peak, top)

    def settle(peak, m_x):
        m_x[...] = jnp.broadcast_to(jnp.max(peak, axis=0, keepdims=True), (8, step))

    def score(kv, b, s_x, d_x, m_x):
        qb = rows_of(q_ref, kv, b)
        gb = rows_of(g_ref, kv, b)
        peak = None
        for lo in range(0, keys, chunk):
            peak = score_chunk(kv, b, lo, qb, gb, s_x, d_x, peak)
        settle(peak, m_x)

    def score_and_backward(kv_s, b_s, s_y, d_y, m_y, kv, b, s_x, d_x, m_x, w_x):
        qb = rows_of(q_ref, kv_s, b_s)
        gb = rows_of(g_ref, kv_s, b_s)
        peak_y = None
        peak = m_x[:1]
        total = jnp.zeros((8, step), F32)
        mixed = jnp.zeros((8, step), F32)
        for lo in range(0, keys, chunk):
            peak_y = score_chunk(kv_s, b_s, lo, qb, gb, s_y, d_y, peak_y)
            for at in range(lo, lo + chunk, fine):
                e = jnp.exp2((s_x[at : at + fine] - peak) * expo)
                s_x[at : at + fine] = e
                total = total + jnp.sum(e.reshape(fine // 8, 8, step), axis=0)
                ed = e * d_x[at : at + fine]
                mixed = mixed + jnp.sum(ed.reshape(fine // 8, 8, step), axis=0)
        settle(peak_y, m_y)
        inverse = 1.0 / jnp.sum(total, axis=0, keepdims=True)
        center = jnp.sum(mixed, axis=0, keepdims=True) * inverse
        here = pl.ds(pl.multiple_of(b * step, step), step)
        dq = None
        for lo in range(0, keys, 256):
            for at in range(lo, lo + 256, fine):
                p = s_x[at : at + fine] * inverse
                p_scr[at : at + fine, here] = p.astype(BF16)
                ds_scr[at : at + fine, here] = (p * (d_x[at : at + fine] - center)).astype(BF16)
            part = tn(ds_scr[lo : lo + 256, here], k_scr[kv, lo : lo + 256])
            dq = part if dq is None else dq + part
        w_x[...] = dq * scale
        rows = pl.ds(pl.multiple_of(b * span, span), span)
        for hh in range(width):
            out = w_x[pl.ds(hh, span, stride=width)].astype(BF16)
            dq_buf[rows, kv * cols + hh * dim : kv * cols + (hh + 1) * dim] = out

    cols = width * dim
    done = 2 * span // piece

    def dq_copy(kv, i):
        to = lax.rem(my_h + i, nh)
        return pltpu.make_async_remote_copy(
            src_ref=dq_buf.at[pl.ds(pl.multiple_of(to * piece, piece), piece), pl.ds(kv * cols, cols)],
            dst_ref=dq_out.at[:, pl.ds(pl.multiple_of(my_h * heads * dim + kv * cols, cols), cols)],
            send_sem=dq_send.at[kv, i - 1],
            recv_sem=dq_recv.at[kv, i - 1],
            device_id={"heads": to},
            device_id_type=MESH,
        )

    def dq_arrival(kv, i):
        source = lax.rem(my_h - i + nh, nh)
        landed = dq_out.at[:, pl.ds(pl.multiple_of(source * heads * dim + kv * cols, cols), cols)]
        return pltpu.make_async_remote_copy(
            src_ref=landed, dst_ref=landed,
            send_sem=dq_send.at[kv, i - 1],
            recv_sem=dq_recv.at[kv, i - 1],
            device_id={"heads": source},
            device_id_type=MESH,
        )

    def dq_own(kv):
        return pltpu.make_async_copy(
            dq_buf.at[pl.ds(pl.multiple_of(my_h * piece, piece), piece), pl.ds(kv * cols, cols)],
            dq_out.at[:, pl.ds(pl.multiple_of(my_h * heads * dim + kv * cols, cols), cols)],
            dq_loc.at[kv],
        )

    def rs_copy(kv, i):
        return pltpu.make_async_remote_copy(
            src_ref=stage.at[kv, i - 1],
            dst_ref=land.at[kv, i - 1],
            send_sem=rs_send.at[kv, i - 1],
            recv_sem=rs_recv.at[kv, i - 1],
            device_id={"dp": lax.rem(my_dp + i, ndp)},
            device_id_type=MESH,
        )

    score(0, 0, s_a, d_a, m_a)
    pl.semaphore_wait(barrier, ndp - 1 + nh - 1)

    for kv in range(kvs):
        def two_blocks(i, c, kv=kv):
            @pl.when(i >= 0)
            def _():
                score_and_backward(
                    kv, 2 * i + 1, s_b, d_b, m_b,
                    kv, 2 * i, s_a, d_a, m_a, w_a,
                )

            @pl.when(i < blocks)
            def _():
                after = kv * blocks + 2 * i + 2
                score_and_backward(
                    jnp.minimum(after // blocks, kvs - 1), lax.rem(after, blocks), s_a, d_a, m_a,
                    kv, 2 * i + 1, s_b, d_b, m_b, w_b,
                )

            for t in range(done):
                away = lax.rem(i * done + t - my_h + nh, nh)

                @pl.when(away == 0)
                def _():
                    dq_own(kv).start()

                @pl.when(away != 0)
                def _():
                    dq_copy(kv, away).start()

            return c

        lax.fori_loop(0, blocks // 2, two_blocks, 0)

        q_rows = q_ref[:, kv * width : (kv + 1) * width, :].reshape(width * tok, dim)
        g_rows = g_ref[:, kv * width : (kv + 1) * width, :].reshape(width * tok, dim)

        def key_block(rows):
            dk = jnp.dot(ds_scr[rows, :], q_rows, preferred_element_type=F32) * scale
            dv = jnp.dot(p_scr[rows, :], g_rows, preferred_element_type=F32)
            return dk, dv

        def send_share(i, c, kv=kv, key_block=key_block):
            to = lax.rem(my_dp + i, ndp)
            dk, dv = key_block(pl.ds(pl.multiple_of(to * share, share), share))
            stage[kv, i - 1, 0] = dk.astype(BF16)
            stage[kv, i - 1, 1] = dv.astype(BF16)
            rs_copy(kv, i).start()
            return c

        lax.fori_loop(1, ndp, send_share, 0)
        dk, dv = key_block(pl.ds(pl.multiple_of(my_dp * share, share), share))
        cart_acc[kv, 0] = dk
        cart_acc[kv, 1] = dv
        dk, dv = key_block(pl.ds(cart, tok))
        self_acc[pl.ds(kv, tok, stride=kvs)] = dk
        self_acc[pl.ds(tok * kvs + kv, tok, stride=kvs)] = dv

    self_out[...] = self_acc[...].astype(BF16)

    for kv in range(kvs):
        dq_own(kv).wait()

        def end_dq(i, c, kv=kv):
            dq_copy(kv, i).wait_send()
            dq_arrival(kv, i).wait_recv()
            return c

        lax.fori_loop(1, nh, end_dq, 0)

        def end_rs(i, c, kv=kv):
            rs_copy(kv, i).wait_send()
            rs_copy(kv, i).wait_recv()
            cart_acc[kv] += land[kv, i - 1].astype(F32)
            return c

        lax.fori_loop(1, ndp, end_rs, 0)
        for kind in range(2):
            cart_out[pl.ds(kind * kvs + kv, share, stride=2 * kvs)] = cart_acc[kv, kind]


def finish(dq_in, cart_in, self_in, dq_out, cart_out, self_out, dq_buf, cart_buf, self_buf, sems):
    trio = ((dq_in, dq_buf, dq_out), (cart_in, cart_buf, cart_out), (self_in, self_buf, self_out))
    for n, (src, buf, _) in enumerate(trio):
        pltpu.make_async_copy(src, buf, sems.at[0, n]).start()
    for n, (src, buf, dst) in enumerate(trio):
        pltpu.make_async_copy(src, buf, sems.at[0, n]).wait()
        pltpu.make_async_copy(buf, dst, sems.at[1, n]).start()
    for n, (_, buf, dst) in enumerate(trio):
        pltpu.make_async_copy(buf, dst, sems.at[1, n]).wait()


def on_device(ndp, nh, queries, out_grad, self_keys, self_values, cart_keys, cart_values, segment_ids):
    tok, heads, dim = queries.shape
    kvs = self_keys.shape[1]
    cart = cart_keys.shape[0]
    keys = cart + tok
    width = heads // kvs
    share = cart // ndp
    piece = tok // nh
    step = 256
    vmem = pl.BlockSpec(memory_space=pltpu.VMEM)
    dma = pltpu.SemaphoreType.DMA
    query_grads, cart_part, self_part = pl.pallas_call(
        functools.partial(kernel, ndp, nh, kvs),
        out_shape=(
            jax.ShapeDtypeStruct((piece, nh * heads * dim), BF16),
            jax.ShapeDtypeStruct((share * 2 * kvs, dim), F32),
            jax.ShapeDtypeStruct((2 * tok * kvs, dim), BF16),
        ),
        in_specs=[vmem] * 7,
        out_specs=(pl.BlockSpec(memory_space=pl.ANY), vmem, vmem),
        scratch_shapes=[
            pltpu.VMEM((tok * width // step, tok, step), F32),
            pltpu.VMEM((kvs, keys, dim), BF16),
            pltpu.VMEM((kvs, keys, dim), BF16),
            pltpu.VMEM((cart * kvs, dim), F32),
            pltpu.VMEM((keys, step), F32),
            pltpu.VMEM((keys, step), F32),
            pltpu.VMEM((8, step), F32),
            pltpu.VMEM((step, dim), F32),
            pltpu.VMEM((keys, step), F32),
            pltpu.VMEM((keys, step), F32),
            pltpu.VMEM((8, step), F32),
            pltpu.VMEM((step, dim), F32),
            pltpu.VMEM((keys, width * tok), BF16),
            pltpu.VMEM((keys, width * tok), BF16),
            pltpu.VMEM((tok, heads * dim), BF16),
            pltpu.VMEM((kvs, ndp - 1, 2, share, dim), BF16),
            pltpu.VMEM((kvs, ndp - 1, 2, share, dim), BF16),
            pltpu.VMEM((kvs, 2, share, dim), F32),
            pltpu.VMEM((2 * tok * kvs, dim), F32),
            dma((kvs, nh - 1)),
            dma((kvs, nh - 1)),
            dma((kvs,)),
            dma((kvs, ndp - 1)),
            dma((kvs, ndp - 1)),
        ],
        compiler_params=pltpu.CompilerParams(
            collective_id=0, has_side_effects=True, vmem_limit_bytes=60 << 20
        ),
        name="attention_backward",
    )(
        segment_ids, queries, out_grad,
        cart_keys.reshape(cart * kvs, dim), cart_values.reshape(cart * kvs, dim),
        self_keys.reshape(tok * kvs, dim), self_values.reshape(tok * kvs, dim),
    )
    parts = (query_grads, cart_part, self_part)
    anywhere = pl.BlockSpec(memory_space=pl.ANY)
    query_grads, cart_part, self_part = pl.pallas_call(
        finish,
        out_shape=tuple(jax.ShapeDtypeStruct(x.shape, x.dtype) for x in parts),
        in_specs=[anywhere] * 3,
        out_specs=(anywhere,) * 3,
        scratch_shapes=[pltpu.VMEM(x.shape, x.dtype) for x in parts] + [dma((2, 3))],
        name="finish",
    )(*parts)
    cart_grads = cart_part.reshape(share, 2, kvs, dim)
    self_grads = self_part.reshape(2, tok, kvs, dim)
    return cart_grads, self_grads, query_grads


def solution(mesh):
    in_specs = (
        P(("groups", "dp"), "heads", None),
        P(("groups", "dp"), "heads", None),
        P(("groups", "dp"), "heads", None),
        P(("groups", "dp"), "heads", None),
        P("groups", "heads", None),
        P("groups", "heads", None),
        P(("groups", "dp"), None),
    )
    out_specs = (
        P(("groups", "dp"), None, "heads", None),
        P(None, ("groups", "dp"), "heads", None),
        P(("groups", "dp", "heads"), None),
    )
    body = functools.partial(on_device, mesh.shape["dp"], mesh.shape["heads"])
    return jax.shard_map(body, mesh=mesh, in_specs=in_specs, out_specs=out_specs, check_vma=False)
```
